32 devices in a mesh: dp: 16 (over z, y, core), fsdp: 2 (over x).
Axes of the slice: x: 2, y: 2, z: 4, core: 2. Of those that a mesh axis runs over, the one named last changes fastest.
Arguments:
- tokens: bfloat16 [16384, 1024], P(('dp', 'fsdp')), may hold values from -6 to 6
- cotangent: bfloat16 [16384, 1024], P(('dp', 'fsdp')), may hold values from -6 to 6
- counts: int32 [32], P(('dp', 'fsdp')), may hold values from 256 to 512, as said below
- segment_ids: int32 [16384], P(('dp', 'fsdp')), may hold values from 0 to 32, as said below
- w_qkv: bfloat16 [1024, 3072], P(('dp', 'fsdp')), may hold values from -0.1875 to 0.1875
- w_out: bfloat16 [1024, 1024], P(('dp', 'fsdp')), may hold values from -0.1875 to 0.1875
- w_fc1: bfloat16 [1024, 4096], P(('dp', 'fsdp')), may hold values from -0.1875 to 0.1875
- w_fc2: bfloat16 [4096, 1024], P(('dp', 'fsdp')), may hold values from -0.09375 to 0.09375
- ln_gains: bfloat16 [3, 1024], P(None, ('dp', 'fsdp')), may hold values from 0.25 to 1.75
- ln_biases: bfloat16 [3, 1024], P(None, ('dp', 'fsdp')), may hold values from -1.796875 to 1.796875
- proj_biases: bfloat16 [4, 1024], P(None, ('dp', 'fsdp')), may hold values from -1.796875 to 1.796875
- ff_gain: bfloat16 [4096], P(('dp', 'fsdp')), may hold values from 0.25 to 1.75
- ff_biases: bfloat16 [2, 4096], P(None, ('dp', 'fsdp')), may hold values from -1.796875 to 1.796875
- head_scale: bfloat16 [16], replicated, may hold values from 0.5 to 2
Outputs:
- layer_out: bfloat16 [16384, 1024], P(('dp', 'fsdp'))
- d_tokens: float32 [16384, 1024], P(('dp', 'fsdp'))
- d_w_qkv: float32 [1024, 3072], P(('dp', 'fsdp'))
- d_w_out: float32 [1024, 1024], P(('dp', 'fsdp'))
- d_w_fc1: float32 [1024, 4096], P(('dp', 'fsdp'))
- d_w_fc2: float32 [4096, 1024], P(('dp', 'fsdp'))
- d_ln_gains: float32 [3, 1024], P(None, ('dp', 'fsdp'))
- d_ln_biases: float32 [3, 1024], P(None, ('dp', 'fsdp'))
- d_proj_biases: float32 [4, 1024], P(None, ('dp', 'fsdp'))
- d_ff_gain: float32 [4096], P(('dp', 'fsdp'))
- d_ff_biases: float32 [2, 4096], P(None, ('dp', 'fsdp'))
- d_head_scale: float32 [16], replicated
The draws below stay inside these ranges and needn't reach their ends.
Inputs may be any that keep to these rules, and one draw needn't show every extreme that they name: `counts`: rows of a device from its count on are unused slots; some device uses all 512 slots and some exactly half of them. `segment_ids`: along each device's 512 rows the ids start at 0 and never fall; a device's unused slots form a segment of their own; on some device all 512 rows are one document; some device reaches the largest id.
All inputs are finite; a program needn't handle non-finite values.
Results may differ from the reference program's by a relative error of at most 0.013.
Values may be sent and summed in bfloat16 or wider, within the bound.
No kernel may reach another device: no remote copies, remote signals or barrier semaphores. Data moves between devices by JAX's collectives and lax.ppermute only.
A program may use at most 256 MiB of HBM per device.

```python
import math
import jax
import jax.numpy as jnp
from jax import lax

HEADS = 16
D = 1024
FF = 4096
TOK_DEV = 512
TOKENS = 16384


def plan_rows(key):
    device_count = TOKENS // TOK_DEV
    id_cap = TOK_DEV // 16
    base_key = jax.random.fold_in(key, 11)
    key_counts, key_order, key_breaks = jax.random.split(base_key, 3)
    used = jax.random.randint(key_counts, (device_count,), TOK_DEV // 2, TOK_DEV + 1)
    order = jax.random.permutation(key_order, device_count)
    device_ids = jnp.arange(device_count)
    used = jnp.where(device_ids == order[0], TOK_DEV, used)
    used = jnp.where(device_ids == order[1], TOK_DEV // 2, used)
    used = jnp.where(device_ids == order[2], 3 * TOK_DEV // 4, used)
    places = jnp.arange(TOK_DEV)[None, :]
    breaks = jax.random.randint(key_breaks, (device_count, TOK_DEV), 0, 160) == 0
    dense_rows = (device_ids == order[2])[:, None] & (places % 8 == 0)
    breaks = (breaks | dense_rows) & (places > 0) & (places < used[:, None]) & (device_ids != order[0])[:, None]
    inner = jnp.minimum(jnp.cumsum(breaks.astype(jnp.int32), axis=1), id_cap - 1)
    segments = (inner + (places >= used[:, None]).astype(jnp.int32)).astype(jnp.int32)
    return (used.astype(jnp.int32), segments.reshape(TOKENS))


def draw_counts(key, part):
    return plan_rows(key)[0]


def draw_segment_ids(key, part):
    return plan_rows(key)[1]


def block_levels(key, extent, cuts, low, high):
    loudness = 1.0
    for dim, shards_of in cuts:
        heights = jax.random.uniform(jax.random.fold_in(jax.random.fold_in(key, 6), dim), (shards_of,), jnp.float32, low / len(cuts), high / len(cuts))
        loudness = loudness * jnp.repeat(jnp.exp(heights), extent[dim] // shards_of).reshape((-1,) + (1,) * (len(extent) - 1 - dim))
    return loudness


def normal_values(own_key, shape, spread, reach, cuts=(), kind=jnp.bfloat16):
    array = jax.random.normal(own_key, shape, jnp.float32) * spread
    if len(cuts) > 0:
        array = block_levels(own_key, shape, cuts, -0.22, 0.18) * array
    return jnp.clip(array, min=-reach, max=reach).astype(kind)


def setup_inputs(seed: int = 0) -> dict:
    arg_keys = jax.random.split(jax.random.key(seed), 15)
    tokens = normal_values(arg_keys[0], (TOKENS, D), 1.0, 6.0, ((0, 32),))
    cotangent = normal_values(arg_keys[1], (TOKENS, D), 1.0, 6.0, ((0, 32),))
    counts = draw_counts(jax.random.fold_in(arg_keys[14], 71), 0)
    segment_ids = draw_segment_ids(jax.random.fold_in(arg_keys[14], 71), 0)
    w_qkv = normal_values(arg_keys[4], (D, 3 * D), D ** -0.5, 0.1875, ((0, 32),))
    w_out = normal_values(arg_keys[5], (D, D), D ** -0.5, 0.1875, ((0, 32),))
    w_fc1 = normal_values(arg_keys[6], (D, FF), D ** -0.5, 0.1875, ((0, 32),))
    w_fc2 = normal_values(arg_keys[7], (FF, D), FF ** -0.5, 0.09375, ((0, 32),))
    ln_gains = jnp.clip(1.0 + 0.15 * jax.random.normal(arg_keys[8], (3, D), jnp.float32), 0.25, 1.75).astype(jnp.bfloat16)
    ln_biases = normal_values(arg_keys[9], (3, D), 0.3, 1.796875, ((1, 32),))
    proj_biases = normal_values(arg_keys[10], (4, D), 0.3, 1.796875, ((1, 32),))
    ff_gain = jnp.clip(1.0 + 0.15 * jax.random.normal(arg_keys[11], (FF,), jnp.float32), 0.25, 1.75).astype(jnp.bfloat16)
    ff_biases = normal_values(arg_keys[12], (2, FF), 0.3, 1.796875, ((1, 32),))
    head_scale = jnp.clip(jnp.exp(jax.random.uniform(arg_keys[13], (HEADS,), jnp.float32, math.log(0.5), math.log(2.0))), 0.5, 2.0).astype(jnp.bfloat16)
    return dict(tokens=tokens, cotangent=cotangent, counts=counts, segment_ids=segment_ids, w_qkv=w_qkv, w_out=w_out, w_fc1=w_fc1, w_fc2=w_fc2, ln_gains=ln_gains, ln_biases=ln_biases, proj_biases=proj_biases, ff_gain=ff_gain, ff_biases=ff_biases, head_scale=head_scale)


@jax.custom_vjp
def low(v):
    return lax.optimization_barrier(v.astype(jnp.bfloat16)).astype(jnp.float32)

@jax.custom_vjp
def low_back(v):
    return v

def low_keep(v):
    return (low(v), None)

def low_pass(kept, grad):
    return (grad,)

def back_keep(v):
    return (v, None)

def back_low(kept, grad):
    return (low(grad),)
low.defvjp(low_keep, low_pass)
low_back.defvjp(back_keep, back_low)

def layer_norm(values, gain_vec, shift_vec):
    center = values - lax.optimization_barrier(jnp.mean(values, -1, keepdims=True))
    inv_std = lax.rsqrt(lax.optimization_barrier(jnp.mean(center * center, -1, keepdims=True)) + 1e-05)
    return center * inv_std * gain_vec + shift_vec

def attention(queries, key_rows, value_rows, segment_ids):
    token_rows, head_count, head_dim = queries.shape
    block_rows = min(512, token_rows)
    blocks = token_rows // block_rows
    factor = head_dim ** (-0.5)

    def one_block(item):
        query_block, seg_block, start_row = item
        scores = low_back(jnp.einsum('qhd,khd->hqk', query_block, key_rows, precision=lax.Precision.HIGHEST) * factor)
        query_pos = start_row + jnp.arange(block_rows, dtype=jnp.int32)
        key_pos = jnp.arange(token_rows, dtype=jnp.int32)
        allowed = (seg_block[:, None] == segment_ids[None, :]) & (key_pos[None, :] <= query_pos[:, None])
        scores = jnp.where(allowed[None], scores, -1e+30)
        shares = low(jax.nn.softmax(scores, axis=-1))
        return low_back(jnp.einsum('hqk,khd->qhd', shares, value_rows, precision=lax.Precision.HIGHEST))
    mapped = lax.map(jax.checkpoint(one_block), (queries.reshape(blocks, block_rows, head_count, head_dim), segment_ids.reshape(blocks, block_rows), jnp.arange(blocks, dtype=jnp.int32) * block_rows))
    return mapped.reshape(token_rows, head_count, head_dim)

def forward(params, inputs, live_rows, segment_ids):
    w_qkv, w_out, w_fc1, w_fc2, ln_gains, ln_biases, proj_biases, ff_gain, ff_biases, head_scale = params
    token_rows, model_width = inputs.shape
    head_count = head_scale.shape[0]
    head_dim = model_width // head_count
    attn_in = low(layer_norm(inputs, ln_gains[0], ln_biases[0]))
    qkv_bias = jnp.concatenate([proj_biases[0], jnp.zeros((model_width,), jnp.float32), proj_biases[1]])
    qkv = low_back(low(jnp.dot(attn_in, w_qkv, precision=lax.Precision.HIGHEST) + qkv_bias))
    queries = qkv[:, :model_width].reshape(token_rows, head_count, head_dim)
    key_rows = qkv[:, model_width:2 * model_width].reshape(token_rows, head_count, head_dim)
    value_rows = qkv[:, 2 * model_width:].reshape(token_rows, head_count, head_dim)
    attended = attention(queries, key_rows, value_rows, segment_ids)
    mixed = low_back(low((attended * head_scale[None, :, None]).reshape(token_rows, model_width)))
    branch = low_back(jnp.dot(mixed, w_out, precision=lax.Precision.HIGHEST) + proj_biases[2])
    residual = inputs + live_rows * layer_norm(branch, ln_gains[1], ln_biases[1])
    ffn_in = low(layer_norm(residual, ln_gains[2], ln_biases[2]))
    hidden = low_back(jnp.dot(ffn_in, w_fc1, precision=lax.Precision.HIGHEST) + ff_biases[0])
    mid_low = low(layer_norm(jax.nn.gelu(hidden, approximate=False), ff_gain, ff_biases[1]))
    second = low_back(jnp.dot(mid_low, w_fc2, precision=lax.Precision.HIGHEST) + proj_biases[3])
    return residual + live_rows * second

def reference(tokens, cotangent, counts, segment_ids, w_qkv, w_out, w_fc1, w_fc2, ln_gains, ln_biases, proj_biases, ff_gain, ff_biases, head_scale):
    device_count = counts.shape[0]
    token_rows = tokens.shape[0] // device_count
    params = tuple((item.astype(jnp.float32) for item in (w_qkv, w_out, w_fc1, w_fc2, ln_gains, ln_biases, proj_biases, ff_gain, ff_biases, head_scale)))
    inputs = tokens.astype(jnp.float32).reshape(device_count, token_rows, D)
    upstream = cotangent.astype(jnp.float32).reshape(device_count, token_rows, D)
    segments = segment_ids.reshape(device_count, token_rows)

    def step(totals, item):
        input_block, grad_block, used_count, seg_block = item
        live_rows = (jnp.arange(token_rows, dtype=jnp.int32) < used_count).astype(jnp.float32)[:, None]
        result, pullback = jax.vjp(lambda weights, values: forward(weights, values, live_rows, seg_block), params, input_block)
        grad_params, grad_input = pullback(grad_block)
        totals = jax.tree.map(lambda left, right: left + right, totals, grad_params)
        return (totals, (result.astype(jnp.bfloat16), grad_input))
    start = jax.tree.map(jnp.zeros_like, params)
    grads, (results, grad_inputs) = lax.scan(step, start, (inputs, upstream, counts, segments))
    return (results.reshape(-1, D), grad_inputs.reshape(-1, D), grads[0], grads[1], grads[2], grads[3], grads[4], grads[5], grads[6], grads[7], grads[8], grads[9])
```

```python
import jax
import jax.numpy as jnp
from jax import lax
from jax.sharding import PartitionSpec as P

AXES = ("dp", "fsdp")
BF = jnp.bfloat16
F32 = jnp.float32


class Grid:
    def __init__(self, dp, fsdp):
        self.Z, self.X = dp // 4, fsdp
        self.n = dp * fsdp
        flat = lax.axis_index(AXES)
        self.x = flat % self.X
        self.c = (flat // self.X) % 2
        self.y = (flat // (2 * self.X)) % 2
        self.z = flat // (4 * self.X)

    def send(self, value, dz=0, dy=0, dc=0, dx=0):
        Z, X = self.Z, self.X
        pairs = []
        for z in range(Z):
            for y in range(2):
                for c in range(2):
                    for x in range(X):
                        src = ((z * 2 + y) * 2 + c) * X + x
                        dst = (((z + dz) % Z * 2 + (y ^ dy)) * 2 + (c ^ dc)) * X + (x + dx) % X
                        pairs.append((src, dst))
        return lax.ppermute(value, AXES, pairs)

    def gather(self, shard):
        Z, X = self.Z, self.X
        r, w = shard.shape
        column = jnp.broadcast_to(shard[None], (Z, r, w))
        for k in range(1, Z):
            column = lax.dynamic_update_slice(column, self.send(shard, dz=k)[None], ((self.z - k) % Z, 0, 0))
        half = Z // 2
        along_x = [self.send(column, dx=k) for k in range(1, X)]
        along_y = self.send(column, dy=1)
        blocks = [(0, 0, 0, column), (0, 1, 0, along_y)]
        for k in range(1, X):
            blocks.append((0, 0, k, along_x[k - 1]))
            blocks.append((0, 1, k, self.send(along_x[k - 1][:half], dy=1)))
            blocks.append((half, 1, k, self.send(along_y[half:], dx=k)))
        whole = jnp.zeros((Z, 2, 2, X, r, w), shard.dtype)
        for cc in range(2):
            for z0, yy, k, block in blocks:
                if cc:
                    block = self.send(block, dc=1)
                spot = (z0, self.y ^ yy, self.c ^ cc, (self.x - k) % X, 0, 0)
                whole = lax.dynamic_update_slice(whole, block[:, None, None, None], spot)
        return whole

    def scatter(self, grad):
        Z, X = self.Z, self.X
        r, w = grad.shape[4:]
        half = Z // 2
        kind = grad.dtype

        def take(c, yy, k):
            start = (0, self.y ^ yy, c, (self.x + k) % X, 0, 0)
            return lax.dynamic_slice(grad, start, (Z, 1, 1, X // X, r, w)).reshape(Z, r, w)

        def add(*terms):
            total = terms[0].astype(F32)
            for term in terms[1:]:
                total = total + term.astype(F32)
            return total.astype(kind)

        sums = {}
        order = [(1, k) for k in range(1, X)] + [(0, k) for k in range(1, X)] + [(1, 0), (0, 0)]
        for yy, k in order:
            other = self.send(take(self.c ^ 1, yy, k), dc=1)
            sums[yy, k] = add(take(self.c, yy, k), other)
        low = [self.send(sums[1, k][:half], dx=k) for k in range(1, X)]
        high = [self.send(sums[1, k][half:], dy=1) for k in range(1, X)]
        own_low, own_high = [sums[0, 0][:half]], [sums[0, 0][half:]]
        own_low.append(self.send(add(sums[1, 0][:half], *low), dy=1))
        own_high.append(self.send(sums[1, 0][half:], dy=1))
        for k in range(1, X):
            own_low.append(self.send(sums[0, k][:half], dx=k))
            own_high.append(self.send(add(sums[0, k][half:], high[k - 1]), dx=k))
        column = jnp.concatenate([add(*own_low), add(*own_high)])
        total = lax.dynamic_index_in_dim(column, self.z, 0, False).astype(F32)
        for k in range(1, Z):
            part = lax.dynamic_index_in_dim(column, (self.z + k) % Z, 0, False)
            total = total + self.send(part, dz=k).astype(F32)
        return total


def layer_norm(values, gain_vec, shift_vec):
    center = values - jnp.mean(values, -1, keepdims=True)
    inv_std = lax.rsqrt(jnp.mean(center * center, -1, keepdims=True) + 1e-05)
    normed = center * inv_std
    return (normed * gain_vec + shift_vec, normed, inv_std)


def norm_back(upstream, gain_vec, normed, inv_std):
    scaled = upstream * gain_vec
    return inv_std * (
        scaled
        - jnp.mean(scaled, -1, keepdims=True)
        - normed * jnp.mean(scaled * normed, -1, keepdims=True)
    )


def gelu_slope(hidden):
    return (
        0.5 * (1.0 + lax.erf(hidden * 0.7071067811865476))
        + hidden * jnp.exp(-0.5 * hidden * hidden) * 0.3989422804014327
    )


def block_scores(queries, key_rows, segment_ids, factor):
    scores = jnp.einsum("qhd,khd->hqk", queries, key_rows, preferred_element_type=F32) * factor
    pos = jnp.arange(segment_ids.shape[0])
    same = segment_ids[:, None] == segment_ids[None, :]
    allowed = same & (pos[None, :] <= pos[:, None])
    return jnp.where(allowed[None], scores, -1e30)


def attend(queries, key_rows, value_rows, segment_ids):
    factor = queries.shape[2] ** (-0.5)
    scores = block_scores(queries, key_rows, segment_ids, factor)
    row_peak = jnp.max(scores, -1, keepdims=True)
    raised = jnp.exp(scores - row_peak)
    denom_sum = jnp.sum(raised, -1, keepdims=True)
    shares_low = (raised / denom_sum).astype(BF)
    log_sum = row_peak + jnp.log(denom_sum)
    pieces = jnp.einsum("hqk,khd->qhd", shares_low, value_rows, preferred_element_type=F32)
    return (pieces, log_sum)


def attend_back(queries, key_rows, value_rows, segment_ids, log_sum, grad_low):
    factor = queries.shape[2] ** (-0.5)
    scores = block_scores(queries, key_rows, segment_ids, factor)
    shares = jnp.exp(scores - log_sum)
    shares_low = shares.astype(BF)
    d_shares = jnp.einsum("qhd,khd->hqk", grad_low, value_rows, preferred_element_type=F32)
    row_inner = jnp.sum(shares * d_shares, -1, keepdims=True)
    d_scores = (shares * (d_shares - row_inner)).astype(BF)
    d_query = jnp.einsum("hqk,khd->qhd", d_scores, key_rows, preferred_element_type=F32) * factor
    d_keys = jnp.einsum("hqk,qhd->khd", d_scores, queries, preferred_element_type=F32) * factor
    d_values = jnp.einsum("hqk,qhd->khd", shares_low, grad_low, preferred_element_type=F32)
    return (d_query, d_keys, d_values)


def body(
    tokens,
    cotangent,
    counts,
    segment_ids,
    w_qkv,
    w_out,
    w_fc1,
    w_fc2,
    ln_gains,
    ln_biases,
    proj_biases,
    ff_gain,
    ff_biases,
    head_scale,
    *,
    dp,
    fsdp,
):
    grid = Grid(dp, fsdp)
    n = grid.n
    token_rows, model_width = tokens.shape
    hidden_width = w_fc1.shape[1]
    rows = model_width // n
    wide = hidden_width // n
    head_count = head_scale.shape[0]
    head_dim = model_width // head_count

    vectors = jnp.concatenate(
        [ln_gains.reshape(-1), ln_biases.reshape(-1), proj_biases.reshape(-1), ff_gain, ff_biases.reshape(-1)]
    )
    small = vectors.shape[0]
    qkv_width = w_qkv.shape[1]
    tail = jnp.pad(vectors[None], ((0, 7), (0, qkv_width - small)))
    first = grid.gather(jnp.concatenate([w_qkv, tail], 0))
    w_qkv_all = first[..., :rows, :].reshape(model_width, qkv_width)
    vectors_all = first[..., rows, :small].reshape(n, small).astype(F32)
    w_out_all = grid.gather(w_out).reshape(model_width, model_width)
    w_fc1_all = grid.gather(w_fc1).reshape(model_width, hidden_width)
    w_fc2_all = grid.gather(w_fc2).reshape(hidden_width, model_width)

    def unpack(offset, count, width):
        part = vectors_all[:, offset : offset + count * width]
        return part.reshape(n, count, width).transpose(1, 0, 2).reshape(count, n * width)

    norm_gains = unpack(0, 3, rows)
    shifts = unpack(3 * rows, 3, rows)
    biases = unpack(6 * rows, 4, rows)
    mid_gain = unpack(10 * rows, 1, wide)[0]
    ffn_biases = unpack(10 * rows + wide, 2, wide)

    inputs = tokens.astype(F32)
    upstream = cotangent.astype(F32)
    live_rows = (jnp.arange(token_rows) < counts[0]).astype(F32)[:, None]
    scale_vec = head_scale.astype(F32)

    first_ln, normed_one, inv_one = layer_norm(inputs, norm_gains[0], shifts[0])
    attn_in = first_ln.astype(BF)
    qkv_bias = jnp.concatenate([biases[0], jnp.zeros((model_width,), F32), biases[1]])
    qkv_low = (jnp.dot(attn_in, w_qkv_all, preferred_element_type=F32) + qkv_bias).astype(BF)
    queries = qkv_low[:, :model_width].reshape(token_rows, head_count, head_dim)
    key_rows = qkv_low[:, model_width : 2 * model_width].reshape(token_rows, head_count, head_dim)
    value_rows = qkv_low[:, 2 * model_width :].reshape(token_rows, head_count, head_dim)
    attended, log_sum = attend(queries, key_rows, value_rows, segment_ids)
    mixed_low = (attended * scale_vec[None, :, None]).reshape(token_rows, model_width).astype(BF)
    branch = jnp.dot(mixed_low, w_out_all, preferred_element_type=F32) + biases[2]
    post_ln, normed_post, inv_post = layer_norm(branch, norm_gains[1], shifts[1])
    residual = inputs + live_rows * post_ln
    second_ln, normed_two, inv_two = layer_norm(residual, norm_gains[2], shifts[2])
    ffn_in = second_ln.astype(BF)
    hidden = jnp.dot(ffn_in, w_fc1_all, preferred_element_type=F32) + ffn_biases[0]
    mid_ln, normed_mid, inv_mid = layer_norm(jax.nn.gelu(hidden, approximate=False), mid_gain, ffn_biases[1])
    mid_low = mid_ln.astype(BF)

    dz_low = (live_rows * upstream).astype(BF)

    def weight_grad(left, right, width):
        grad = jnp.einsum("td,te->de", left, right, preferred_element_type=F32).astype(BF)
        return grid.scatter(grad.reshape(grid.Z, 2, 2, grid.X, width, right.shape[1]))

    d_fc2 = weight_grad(mid_low, dz_low, wide)
    result = residual + live_rows * (jnp.dot(mid_low, w_fc2_all, preferred_element_type=F32) + biases[3])
    layer_out = result.astype(BF)
    d_fc2_bias = jnp.sum(dz_low.astype(F32), 0)
    d_mid = jnp.einsum("td,fd->tf", dz_low, w_fc2_all, preferred_element_type=F32)
    d_mid_gain = jnp.sum(d_mid * normed_mid, 0)
    d_mid_bias = jnp.sum(d_mid, 0)
    d_gelu = norm_back(d_mid, mid_gain, normed_mid, inv_mid)
    dh_low = (d_gelu * gelu_slope(hidden)).astype(BF)
    d_fc1 = weight_grad(ffn_in, dh_low, rows)
    d_fc1_bias = jnp.sum(dh_low.astype(F32), 0)
    d_second = jnp.einsum("tf,df->td", dh_low, w_fc1_all, preferred_element_type=F32)
    d_gain_two = jnp.sum(d_second * normed_two, 0)
    d_shift_two = jnp.sum(d_second, 0)
    d_resid = upstream + norm_back(d_second, norm_gains[2], normed_two, inv_two)
    d_post = live_rows * d_resid
    d_gain_post = jnp.sum(d_post * normed_post, 0)
    d_shift_post = jnp.sum(d_post, 0)
    dy_low = norm_back(d_post, norm_gains[1], normed_post, inv_post).astype(BF)
    d_out = weight_grad(mixed_low, dy_low, rows)
    d_out_bias = jnp.sum(dy_low.astype(F32), 0)
    dao_low = jnp.einsum("td,cd->tc", dy_low, w_out_all, preferred_element_type=F32).astype(BF)
    dao_heads = dao_low.astype(F32).reshape(token_rows, head_count, head_dim)
    d_scale = jnp.sum(dao_heads * attended, axis=(0, 2))
    do_low = (dao_heads * scale_vec[None, :, None]).astype(BF)
    d_query, d_key, d_value = attend_back(queries, key_rows, value_rows, segment_ids, log_sum, do_low)
    dqkv_low = jnp.concatenate(
        [part.reshape(token_rows, model_width) for part in (d_query, d_key, d_value)], 1
    ).astype(BF)
    d_qkv = weight_grad(attn_in, dqkv_low, rows)
    dqkv_wide = dqkv_low.astype(F32)
    d_query_bias = jnp.sum(dqkv_wide[:, :model_width], 0)
    d_value_bias = jnp.sum(dqkv_wide[:, 2 * model_width :], 0)
    d_first = jnp.einsum("te,de->td", dqkv_low, w_qkv_all, preferred_element_type=F32)
    d_gain_one = jnp.sum(d_first * normed_one, 0)
    d_shift_one = jnp.sum(d_first, 0)
    d_inputs = d_resid + norm_back(d_first, norm_gains[0], normed_one, inv_one)

    narrow = jnp.stack(
        [
            d_gain_one,
            d_gain_post,
            d_gain_two,
            d_shift_one,
            d_shift_post,
            d_shift_two,
            d_query_bias,
            d_value_bias,
            d_out_bias,
            d_fc2_bias,
        ]
    )
    broad = jnp.stack([d_mid_gain, d_fc1_bias, d_mid_bias])
    packed = jnp.concatenate(
        [
            narrow.reshape(10, n, rows).transpose(1, 0, 2).reshape(n, 10 * rows),
            broad.reshape(3, n, wide).transpose(1, 0, 2).reshape(n, 3 * wide),
            jnp.broadcast_to(d_scale[None], (n, head_count)),
        ],
        1,
    )
    length = packed.shape[1]
    room = -(-length // 1024) * 1024
    packed = jnp.pad(packed, ((0, 0), (0, room - length)))
    totals = grid.scatter(packed.reshape(grid.Z, 2, 2, grid.X, room // 128, 128)).reshape(-1)
    d_narrow = totals[: 10 * rows].reshape(10, rows)
    d_broad = totals[10 * rows : 10 * rows + 3 * wide].reshape(3, wide)
    scale_total = totals[10 * rows + 3 * wide : length]
    return (
        layer_out,
        d_inputs,
        d_qkv,
        d_out,
        d_fc1,
        d_fc2,
        d_narrow[0:3],
        d_narrow[3:6],
        d_narrow[6:10],
        d_broad[0],
        d_broad[1:3],
        scale_total,
    )


def solution(mesh):
    rows = P(AXES, None)
    flat = P(AXES)
    lanes = P(None, AXES)

    def step(*args):
        return body(*args, dp=mesh.shape["dp"], fsdp=mesh.shape["fsdp"])

    return jax.shard_map(
        step,
        mesh=mesh,
        in_specs=(rows, rows, flat, flat, rows, rows, rows, rows, lanes, lanes, lanes, flat, lanes, P()),
        out_specs=(rows, rows, rows, rows, rows, rows, lanes, lanes, lanes, flat, lanes, P()),
        check_vma=False,
    )
```
